32 devices in a mesh: dp: 4 (over y, core), seq: 8 (over z, x).
Axes of the slice: x: 2, y: 2, z: 4, core: 2. Of those that a mesh axis runs over, the one named last changes fastest.
Arguments:
- activations: bfloat16 [8, 2048, 1536], P('dp', 'seq'), may hold values from -6 to 6
- gate_weight: bfloat16 [1536, 3072], P(('dp', 'seq')), may hold values from -0.15625 to 0.15625
- mixer_weight: bfloat16 [1536, 3328], P(('dp', 'seq')), may hold values from -0.15625 to 0.15625
- step_weight: bfloat16 [1536, 48], P(('dp', 'seq')), may hold values from -0.15625 to 0.15625
- out_weight: bfloat16 [3072, 1536], P(('dp', 'seq')), may hold values from -0.109375 to 0.109375
- conv_weight: bfloat16 [4, 3328], P(None, ('dp', 'seq')), may hold values from -3 to 3
- conv_bias: bfloat16 [3328], P(('dp', 'seq')), may hold values from -0.5 to 0.5
- norm_gain: bfloat16 [1536], P(('dp', 'seq')), may hold values from 0.099609375 to 1.8984375
- gate_gain: bfloat16 [3072], P(('dp', 'seq')), may hold values from 0.099609375 to 1.8984375
- step_bias: float32 [48], replicated, may hold values from -4.5 to -3.5
- decay_log: float32 [48], replicated, may hold values from -8 to 4
- skip_gain: float32 [48], replicated, may hold values from 0.5 to 2
- cotangent: bfloat16 [8, 2048, 1536], P('dp', 'seq'), may hold values from -6 to 6
Outputs:
- output: bfloat16 [8, 2048, 1536], P('dp', 'seq')
- input_grad: float32 [8, 2048, 1536], P('dp', 'seq')
- gate_weight_grad: float32 [1536, 3072], P(('dp', 'seq'))
- mixer_weight_grad: float32 [1536, 3328], P(('dp', 'seq'))
- step_weight_grad: float32 [1536, 48], P(('dp', 'seq'))
- out_weight_grad: float32 [3072, 1536], P(('dp', 'seq'))
- conv_weight_grad: float32 [4, 3328], P(None, ('dp', 'seq'))
- conv_bias_grad: float32 [3328], P(('dp', 'seq'))
- norm_gain_grad: float32 [1536], P(('dp', 'seq'))
- gate_gain_grad: float32 [3072], P(('dp', 'seq'))
- step_bias_grad: float32 [48], replicated
- decay_log_grad: float32 [48], replicated
- skip_gain_grad: float32 [48], replicated
The draws below stay inside these ranges and needn't reach their ends.
All inputs are finite; a program needn't handle non-finite values.
Results may differ from the reference program's by a relative error of at most 0.012.
Values may be sent and summed in bfloat16 or wider, within the bound.
No kernel may reach another device: no remote copies, remote signals or barrier semaphores. Data moves between devices by JAX's collectives and lax.ppermute only.
A program may use at most 256 MiB of HBM per device.

```python
import jax
import jax.numpy as jnp
from jax import lax

D = 1536
HEADS = 48
HDIM = 64
STATE = 128
KCONV = 4
BLOCK = 256
INNER = 3072
CONVCH = 3328
SEQS = 8
SEQLEN = 2048


def draw_decay_log(key, part):
    shuffled = jax.random.permutation(jax.random.fold_in(key, 11), HEADS)
    slow_count = HEADS // 2
    slow_heads = shuffled < slow_count
    spread = jax.random.uniform(jax.random.fold_in(key, 12), (HEADS,), jnp.float32)
    slow_rate = (0.3 + 1.2 * spread) / SEQLEN
    fast_rate = (5.0 + 3.0 * spread) / BLOCK
    step_rate = jnp.where(slow_heads, slow_rate, fast_rate)
    return jnp.log(step_rate / 0.03).astype(jnp.float32)


def block_levels(own_key, dims, shards, least, high):
    factor_of, own = 1.0, jax.random.fold_in(own_key, 6)
    for axis_at, blocks in shards:
        steps = jnp.exp(jax.random.uniform(jax.random.fold_in(own, axis_at), (blocks,), jnp.float32, least / len(shards), high / len(shards)))
        factor_of = factor_of * jnp.repeat(steps, dims[axis_at] // blocks).reshape([-1 if axis == axis_at else 1 for axis in range(len(dims))])
    return factor_of


def bell_draw(key, dims, deviation, bound, shards=(), kind=jnp.bfloat16):
    factor_of = block_levels(key, dims, shards, -0.22, 0.18) if shards else 1.0
    drawn = jax.random.normal(key, dims, jnp.float32) * deviation * factor_of
    return jnp.minimum(jnp.maximum(drawn, -bound), bound).astype(kind)


def setup_inputs(seed: int = 0) -> dict:
    key_list = jax.random.split(jax.random.key(seed), 14)
    activations = bell_draw(key_list[0], (SEQS, SEQLEN, D), 1.0, 6.0, ((0, 4), (1, 8)))
    gate_weight = bell_draw(key_list[1], (D, INNER), D ** -0.5, 0.15625, ((0, 32),))
    mixer_weight = bell_draw(key_list[2], (D, CONVCH), D ** -0.5, 0.15625, ((0, 32),))
    step_weight = bell_draw(key_list[3], (D, HEADS), D ** -0.5, 0.15625, ((0, 32),))
    out_weight = bell_draw(key_list[4], (INNER, D), INNER ** -0.5, 0.109375, ((0, 32),))
    conv_weight = bell_draw(key_list[5], (KCONV, CONVCH), KCONV ** -0.5, 3.0, ((1, 32),))
    conv_bias = jnp.clip(jax.random.uniform(key_list[6], (CONVCH,), jnp.float32, -0.5, 0.5) * block_levels(key_list[6], (CONVCH,), ((0, 32),), -0.4, 0.0), -0.5, 0.5).astype(jnp.bfloat16)
    norm_gain = jnp.clip(1.0 + 0.18 * jax.random.normal(key_list[7], (D,), jnp.float32), 0.099609375, 1.8984375).astype(jnp.bfloat16)
    gate_gain = jnp.clip(1.0 + 0.18 * jax.random.normal(key_list[8], (INNER,), jnp.float32), 0.099609375, 1.8984375).astype(jnp.bfloat16)
    step_bias = jnp.clip(jax.random.uniform(key_list[9], (HEADS,), jnp.float32, -4.5, -3.5), -4.5, -3.5)
    decay_log = draw_decay_log(jax.random.fold_in(key_list[13], 71), 0)
    skip_gain = jnp.clip(jax.random.uniform(key_list[11], (HEADS,), jnp.float32, 0.5, 2.0), 0.5, 2.0)
    cotangent = bell_draw(key_list[12], (SEQS, SEQLEN, D), 1.0, 6.0, ((0, 4), (1, 8)))
    return dict(activations=activations, gate_weight=gate_weight, mixer_weight=mixer_weight, step_weight=step_weight, out_weight=out_weight, conv_weight=conv_weight, conv_bias=conv_bias, norm_gain=norm_gain, gate_gain=gate_gain, step_bias=step_bias, decay_log=decay_log, skip_gain=skip_gain, cotangent=cotangent)


@jax.custom_vjp
def low(v):
    return lax.optimization_barrier(v.astype(jnp.bfloat16)).astype(jnp.float32)

@jax.custom_vjp
def low_back(v):
    return v

def low_keep(v):
    return (low(v), None)

def low_pass(kept, grad):
    return (grad,)

def back_keep(v):
    return (v, None)

def back_low(kept, grad):
    return (low(grad),)
low.defvjp(low_keep, low_pass)
low_back.defvjp(back_keep, back_low)
precise = lax.Precision.HIGHEST
epsilon = 1e-05

def matmul(left, right):
    return jnp.dot(left, right, precision=precise, preferred_element_type=jnp.float32)

def rounded(value):
    return low_back(low(value))

def mixer_block(carry_state, pieces):
    values, inputs_b, inputs_c, step_sizes, log_decay = pieces
    length = log_decay.shape[0]
    cumulative = jnp.cumsum(log_decay, axis=0)
    row_ids = lax.broadcasted_iota(jnp.int32, (length, length), 0)
    col_ids = lax.broadcasted_iota(jnp.int32, (length, length), 1)
    causal = (row_ids >= col_ids)[:, :, None]
    differ = cumulative[:, None, :] - cumulative[None, :, :]
    segment = jnp.where(causal, jnp.exp(jnp.where(causal, differ, 0.0)), 0.0)
    scores = matmul(rounded(inputs_c), rounded(inputs_b).T)
    mixing = rounded(segment * scores[:, :, None] * step_sizes[None, :, :])
    inside = jnp.einsum('ijh,jhp->ihp', mixing, rounded(values), precision=precise)
    carried = jnp.einsum('in,hpn->ihp', rounded(inputs_c), rounded(carry_state), precision=precise) * jnp.exp(cumulative)[:, :, None]
    to_end = jnp.exp(cumulative[-1][None, :] - cumulative) * step_sizes
    fresh_part = jnp.einsum('jhp,jn->hpn', rounded(values * to_end[:, :, None]), rounded(inputs_b), precision=precise)
    new_state = jnp.exp(cumulative[-1])[:, None, None] * carry_state + fresh_part
    return (new_state, inside + carried)

def forward(source, gate_weight, mixer_weight, step_weight, out_weight, conv_weight, conv_bias, norm_gain, gate_gain, step_bias, decay_log, skip_gain):
    scaling = lax.rsqrt(lax.optimization_barrier(jnp.mean(source * source, axis=-1, keepdims=True)) + epsilon)
    normed = low(source * scaling * norm_gain)
    gate_z = low_back(matmul(normed, gate_weight))
    mixed_in = low_back(matmul(normed, mixer_weight))
    raw_dt = low_back(matmul(normed, step_weight))
    padded = jnp.concatenate([jnp.zeros((KCONV - 1, CONVCH), jnp.float32), mixed_in], axis=0)
    convolved = conv_bias + conv_weight[0] * padded[0:SEQLEN]
    for offset in range(1, KCONV):
        convolved = convolved + conv_weight[offset] * padded[offset:offset + SEQLEN]
    active = jax.nn.silu(convolved)
    values = active[:, :INNER].reshape(SEQLEN, HEADS, HDIM)
    inputs_b = active[:, INNER:INNER + STATE]
    inputs_c = active[:, INNER + STATE:]
    step_sizes = jax.nn.softplus(raw_dt + step_bias)
    log_decay = -jnp.exp(decay_log) * step_sizes
    num_blocks = SEQLEN // BLOCK

    def blocked(array):
        return array.reshape((num_blocks, BLOCK) + array.shape[1:])
    initial = jnp.zeros((HEADS, HDIM, STATE), jnp.float32)
    final_state, pieces_out = lax.scan(jax.checkpoint(mixer_block), initial, (blocked(values), blocked(inputs_b), blocked(inputs_c), blocked(step_sizes), blocked(log_decay)))
    mixed_out = pieces_out.reshape(SEQLEN, HEADS, HDIM) + skip_gain[None, :, None] * values
    gated_out = mixed_out.reshape(SEQLEN, INNER) * jax.nn.silu(gate_z)
    scaling_gate = lax.rsqrt(lax.optimization_barrier(jnp.mean(gated_out * gated_out, axis=-1, keepdims=True)) + epsilon)
    gnorm = low(gated_out * scaling_gate * gate_gain)
    return source + matmul(gnorm, out_weight)

def reference(activations, gate_weight, mixer_weight, step_weight, out_weight, conv_weight, conv_bias, norm_gain, gate_gain, step_bias, decay_log, skip_gain, cotangent):
    weights = tuple((array.astype(jnp.float32) for array in (gate_weight, mixer_weight, step_weight, out_weight, conv_weight, conv_bias, norm_gain, gate_gain, step_bias, decay_log, skip_gain)))

    def one_sequence(totals, seq_items):
        source, tangent = seq_items
        result, pullback = jax.vjp(forward, source.astype(jnp.float32), *weights)
        local_grads = pullback(tangent.astype(jnp.float32))
        new_totals = tuple((total + grad for total, grad in zip(totals, local_grads[1:])))
        return (new_totals, (result.astype(jnp.bfloat16), local_grads[0]))
    initial = tuple((jnp.zeros_like(array) for array in weights))
    totals, (results, input_grads) = lax.scan(one_sequence, initial, (activations, cotangent))
    return (results, input_grads, totals[0], totals[1], totals[2], totals[3], totals[4], totals[5], totals[6], totals[7], totals[8], totals[9], totals[10])
```

```python
import functools

import jax
import jax.numpy as jnp
from jax import lax
from jax.experimental import pallas as pl
from jax.experimental.pallas import tpu as pltpu
from jax.sharding import PartitionSpec as P

HEADS = 48
HDIM = 64
STATE = 128
KCONV = 4
INNER = 3072
CONVCH = 3328
PACKED = 3456
LB = 256
NB = INNER // LB
HB = LB // HDIM

F32 = jnp.float32
BF16 = jnp.bfloat16
precise = lax.Precision.HIGHEST
epsilon = 1e-05


class Grid:
    def __init__(self):
        self.dp = lax.axis_size("dp")
        self.seq = lax.axis_size("seq")
        self.size = {"c": 2, "y": self.dp // 2}
        across = self.size["y"] if self.seq % max(self.size["y"], 1) == 0 else 1
        self.size["x"] = across
        self.size["z"] = self.seq // across
        d, s = lax.axis_index("dp"), lax.axis_index("seq")
        self.at = {"c": d % 2, "y": d // 2, "x": s % across, "z": s // across}

    def pairs(self, move):
        found = []
        for d in range(self.dp):
            for s in range(self.seq):
                place = {"c": d % 2, "y": d // 2, "x": s % self.size["x"], "z": s // self.size["x"]}
                to = move(dict(place))
                if to is None:
                    continue
                dd = to["y"] * 2 + to["c"]
                ss = to["z"] * self.size["x"] + to["x"]
                found.append((d * self.seq + s, dd * self.seq + ss))
        return found

    def rotate(self, value, axis, by):
        count = self.size[axis]

        def move(place):
            place[axis] = (place[axis] + by) % count
            return place

        return lax.ppermute(value, ("dp", "seq"), self.pairs(move))

    def flip(self, value, axis, bit):
        def move(place):
            place[axis] = place[axis] ^ bit
            return place

        return lax.ppermute(value, ("dp", "seq"), self.pairs(move))

    def step(self, value, axis, by):
        count = self.size[axis]

        def move(place):
            place[axis] = place[axis] + by
            return place if 0 <= place[axis] < count else None

        return lax.ppermute(value, ("dp", "seq"), self.pairs(move))


def shifted(x, axis, by):
    peers = lax.axis_size(axis)
    pairs = [(i, i + by) for i in range(peers) if 0 <= i + by < peers]
    return lax.ppermute(x, axis, pairs)


def reduce_axis(grid, value, axis, place, last=False):
    count = grid.size[axis]
    here = grid.at[axis]
    total = lax.dynamic_index_in_dim(value, here, place, False).astype(F32)
    for by in range(1, count):
        sent = lax.dynamic_index_in_dim(value, (here + by) % count, place, False)
        total = total + grid.rotate(sent, axis, by).astype(F32)
    return total if last else total.astype(BF16)


def scatter_sum(grid, make, rows, width):
    core = grid.at["c"]
    dims = (grid.size["y"], grid.size["z"], grid.size["x"], rows, width)
    arrived = grid.rotate(make(1 - core).astype(BF16), "c", 1)
    kept = (make(core) + arrived.astype(F32)).astype(BF16).reshape(dims)
    cut = (width // 256) * 128
    left, right = kept[..., :cut], kept[..., cut:]
    left = reduce_axis(grid, left, "x", 2)
    right = reduce_axis(grid, right, "y", 0)
    left = reduce_axis(grid, left, "y", 0)
    right = reduce_axis(grid, right, "x", 1)
    return reduce_axis(grid, jnp.concatenate([left, right], axis=-1), "z", 0, last=True)


def total_of(grid, value):
    for axis in ("c", "x", "y", "z"):
        bit = 1
        while bit < grid.size[axis]:
            value = value + grid.flip(value, axis, bit)
            bit *= 2
    return value


def carried_in(grid, fresh, decay, reverse):
    across, deep = grid.size["x"], grid.size["z"]
    x, z = grid.at["x"], grid.at["z"]
    lanes = fresh.shape[-1] // across
    by_part = fresh.reshape(fresh.shape[0], across, lanes)
    decay_parts = decay.reshape(1, across, lanes)

    def swap(parts):
        got = [None] * across
        own = lax.dynamic_index_in_dim(parts, x, 1, False)
        out = jnp.zeros((across,) + own.shape, own.dtype)
        out = lax.dynamic_update_index_in_dim(out, own, x, 0)
        for by in range(1, across):
            sent = lax.dynamic_index_in_dim(parts, (x + by) % across, 1, False)
            out = lax.dynamic_update_index_in_dim(out, grid.rotate(sent, "x", by), (x - by) % across, 0)
        return out

    blocks = swap(by_part)
    decays = swap(decay_parts)
    order = list(range(across))
    if reverse:
        order = order[::-1]
    whole, through = None, None
    for b in order:
        here = blocks[b].astype(F32)
        whole = here if whole is None else whole * decays[b] + here
        through = decays[b] if through is None else through * decays[b]
    entering = jnp.zeros(whole.shape, BF16)
    moved = None
    for lap in range(deep - 1):
        leaving = whole if moved is None else moved.astype(F32) * through + whole
        moved = grid.step(leaving.astype(BF16), "z", -1 if reverse else 1)
    state = entering.astype(F32) if moved is None else moved.astype(F32)
    entered = [None] * across
    for b in order:
        entered[b] = state.astype(BF16)
        state = state * decays[b] + blocks[b].astype(F32)
    stacked = jnp.stack(entered, axis=0)
    own = lax.dynamic_index_in_dim(stacked, x, 0, False)
    out = jnp.zeros((fresh.shape[0], across, lanes), BF16)
    out = lax.dynamic_update_index_in_dim(out, own, x, 1)
    for by in range(1, across):
        sent = lax.dynamic_index_in_dim(stacked, (x + by) % across, 0, False)
        out = lax.dynamic_update_index_in_dim(out, grid.rotate(sent, "x", by), (x - by) % across, 1)
    return out.reshape(fresh.shape)


def mm(left, right):
    return jnp.dot(left, right, preferred_element_type=F32)


def mm_nt(left, right):
    return lax.dot_general(left, right, (((1,), (1,)), ((), ())), preferred_element_type=F32)


def spread(value, table):
    high = value.astype(BF16)
    low = (value - high.astype(F32)).astype(BF16)
    return mm(high, table) + mm(low, table)


def sigmoid(v):
    return 1.0 / (1.0 + jnp.exp(-v))


def convolve(mixed, edge, taps, bias):
    length = mixed.shape[0]
    ext = jnp.concatenate([edge, mixed], axis=0)
    base = edge.shape[0] - KCONV + 1
    out = bias + taps[0:1] * ext[base : base + length]
    for k in range(1, KCONV):
        out = out + taps[k : k + 1] * ext[base + k : base + k + length]
    return out, ext


def front_kernel(mixed, edge, taps, bias, weigh, table, active, state, bt):
    g = pl.program_id(1)
    conv, _ = convolve(mixed[0], edge[0], taps[...], bias[...])
    act = conv * sigmoid(conv)
    active[0] = act.astype(BF16)

    @pl.when(g == 0)
    def _():
        bt[...] = act[:, :STATE].astype(BF16).T

    @pl.when(g > 0)
    def _():
        weighted = (act * spread(weigh[0], table[...])).astype(BF16)
        state[0] = mm(bt[...], weighted).astype(BF16)


def front(mixed, edge, taps, bias, weigh, table):
    seqs, length, _ = weigh.shape
    first = lambda g: lax.rem(g + NB, NB + 1)
    after = lambda g: jnp.maximum(g - 1, 0)
    return pl.pallas_call(
        front_kernel,
        grid=(seqs, NB + 1),
        in_specs=[
            pl.BlockSpec((1, length, LB), lambda s, g: (s, 0, first(g))),
            pl.BlockSpec((1, 8, LB), lambda s, g: (s, 0, first(g))),
            pl.BlockSpec((KCONV, LB), lambda s, g: (0, first(g))),
            pl.BlockSpec((1, LB), lambda s, g: (0, first(g))),
            pl.BlockSpec((1, length, HEADS), lambda s, g: (s, 0, 0)),
            pl.BlockSpec((HEADS, LB), lambda s, g: (0, after(g))),
        ],
        out_specs=[
            pl.BlockSpec((1, length, LB), lambda s, g: (s, 0, first(g))),
            pl.BlockSpec((1, STATE, LB), lambda s, g: (s, 0, after(g))),
        ],
        out_shape=[
            jax.ShapeDtypeStruct((seqs, length, CONVCH), BF16),
            jax.ShapeDtypeStruct((seqs, STATE, INNER), BF16),
        ],
        scratch_shapes=[pltpu.VMEM((STATE, length), BF16)],
        cost_estimate=pl.CostEstimate(flops=2 * 10**9, bytes_accessed=12 * 10**6, transcendentals=2 * 10**6),
        name="front",
    )(mixed, edge, taps, bias, weigh, table)


def inside_kernel(values, bc, lcol, lrow, srow, skip, own, scores):
    g = pl.program_id(1)
    length = values.shape[1]
    half = length // 2

    @pl.when(g == 0)
    def _():
        scores[...] = mm_nt(bc[0][:, STATE:], bc[0][:, :STATE])

    low_lane = lax.broadcasted_iota(jnp.int32, (length, 128), 1) < HDIM
    causal = lax.broadcasted_iota(jnp.int32, (half, half), 0) >= lax.broadcasted_iota(jnp.int32, (half, half), 1)
    for pair in range(HB // 2):
        lanes = slice(pair * 128, pair * 128 + 128)
        x = values[0][:, lanes]
        top = jnp.zeros((half, 128), F32)
        bottom = jnp.zeros((half, 128), F32)
        for side in range(2):
            h = 2 * pair + side
            mine = jnp.where(low_lane if side == 0 else jnp.logical_not(low_lane), x, jnp.zeros_like(x))
            lc, lr, sr = lcol[0, 0][:, h : h + 1], lrow[0, 0][h : h + 1], srow[0, 0][h : h + 1]

            def mix(rows, cols, masked):
                differ = lc[rows] - lr[:, cols]
                if masked:
                    differ = jnp.where(causal, differ, -1e30)
                return (jnp.exp(differ) * scores[rows, cols] * sr[:, cols]).astype(BF16)

            a, b = slice(0, half), slice(half, length)
            top = top + mm(mix(a, a, True), mine[:half])
            bottom = bottom + mm(mix(b, a, False), mine[:half]) + mm(mix(b, b, True), mine[half:])
        xs = x.astype(F32) * skip[:, lanes]
        own[0, :half, lanes] = (top + xs[:half]).astype(BF16)
        own[0, half:, lanes] = (bottom + xs[half:]).astype(BF16)


def inside(active, lcol, lrow, srow, skip):
    seqs, length, _ = active.shape
    return pl.pallas_call(
        inside_kernel,
        grid=(seqs, NB),
        in_specs=[
            pl.BlockSpec((1, length, LB), lambda s, g: (s, 0, g)),
            pl.BlockSpec((1, length, LB), lambda s, g: (s, 0, NB)),
            pl.BlockSpec((1, 1, length, HB), lambda s, g: (s, g, 0, 0)),
            pl.BlockSpec((1, 1, HB, length), lambda s, g: (s, g, 0, 0)),
            pl.BlockSpec((1, 1, HB, length), lambda s, g: (s, g, 0, 0)),
            pl.BlockSpec((1, LB), lambda s, g: (0, g)),
        ],
        out_specs=pl.BlockSpec((1, length, LB), lambda s, g: (s, 0, g)),
        out_shape=jax.ShapeDtypeStruct((seqs, length, INNER), BF16),
        scratch_shapes=[pltpu.VMEM((length, length), F32)],
        cost_estimate=pl.CostEstimate(flops=20 * 10**9, bytes_accessed=8 * 10**6, transcendentals=6 * 10**6),
        name="inside",
    )(active, active, lcol, lrow, srow, skip)


def gate_kernel(own, gate_z, top, c, state, grown, table, folded, gain, gnorm, gate_grad, mixed_grad, entry, carry_grad, gain_grad):
    first = (pl.program_id(0) == 0) & (pl.program_id(1) == 0)
    wide = spread(grown[0], table[...])
    carried = mm(c[0], state[0]) * wide
    mixed = own[0].astype(F32) + carried
    z = gate_z[0]
    s = sigmoid(z)
    sl = z * s
    gated = mixed * sl
    scale = lax.rsqrt(jnp.mean(gated * gated, axis=-1, keepdims=True) + epsilon)
    u = gated * scale
    gnorm[0] = (u * gain[...]).astype(BF16)
    upper = top[0]
    t = upper * gain[...]
    grad = scale * (t - u * jnp.mean(t * u, axis=-1, keepdims=True))
    part = jnp.sum(upper * u, axis=0, keepdims=True)

    @pl.when(first)
    def _():
        gain_grad[...] = part

    @pl.when(jnp.logical_not(first))
    def _():
        gain_grad[...] += part

    gate_grad[0] = (grad * mixed * (s * (1.0 + z * (1.0 - s)))).astype(BF16)
    mg = grad * sl
    mixed_grad[0] = mg.astype(BF16)
    entry[0] = (mg * wide).astype(BF16)
    carry_grad[0] = spread(mg * carried, folded[...])


def gate(own, gate_z, top, active, state, grown, table, folded, gain):
    seqs, length, _ = own.shape
    tr = 64
    wide = pl.BlockSpec((1, tr, INNER), lambda s, r: (s, r, 0))
    shape = jax.ShapeDtypeStruct((seqs, length, INNER), BF16)
    return pl.pallas_call(
        gate_kernel,
        grid=(seqs, length // tr),
        in_specs=[
            wide,
            wide,
            wide,
            pl.BlockSpec((1, tr, STATE), lambda s, r: (s, r, (INNER + STATE) // STATE)),
            pl.BlockSpec((1, STATE, INNER), lambda s, r: (s, 0, 0)),
            pl.BlockSpec((1, tr, HEADS), lambda s, r: (s, r, 0)),
            pl.BlockSpec((HEADS, INNER), lambda s, r: (0, 0)),
            pl.BlockSpec((INNER, HEADS), lambda s, r: (0, 0)),
            pl.BlockSpec((1, INNER), lambda s, r: (0, 0)),
        ],
        out_specs=[
            wide,
            wide,
            wide,
            wide,
            pl.BlockSpec((1, tr, HEADS), lambda s, r: (s, r, 0)),
            pl.BlockSpec((1, INNER), lambda s, r: (0, 0)),
        ],
        out_shape=[
            shape,
            shape,
            shape,
            shape,
            jax.ShapeDtypeStruct((seqs, length, HEADS), F32),
            jax.ShapeDtypeStruct((1, INNER), F32),
        ],
        cost_estimate=pl.CostEstimate(flops=2 * 10**9, bytes_accessed=30 * 10**6, transcendentals=2 * 10**6),
        name="gated",
    )(own, gate_z, top, active, state, grown, table, folded, gain)


def local_kernel(values, grads, bc, lcol, lrow, scol, skip, value_grad, row_sum, col_sum, b_grad, c_grad, skip_grad, scores, scores_grad):
    g = pl.program_id(1)
    length = values.shape[1]
    half = length // 2

    @pl.when(g == 0)
    def _():
        scores[...] = mm_nt(bc[0][:, :STATE], bc[0][:, STATE:])
        scores_grad[...] = jnp.zeros_like(scores_grad)

    low_lane = lax.broadcasted_iota(jnp.int32, (length, 128), 1) < HDIM
    causal = lax.broadcasted_iota(jnp.int32, (half, half), 0) <= lax.broadcasted_iota(jnp.int32, (half, half), 1)
    a, b = slice(0, half), slice(half, length)
    for pair in range(HB // 2):
        lanes = slice(pair * 128, pair * 128 + 128)
        x, dy = values[0][:, lanes], grads[0][:, lanes]
        dyf = dy.astype(F32)
        xf = x.astype(F32)
        skip_grad[0, :, lanes] = jnp.sum(dyf * xf, axis=0, keepdims=True)
        upper = jnp.zeros((half, 128), F32)
        lower = jnp.zeros((half, 128), F32)
        for side in range(2):
            h = 2 * pair + side
            keep = low_lane if side == 0 else jnp.logical_not(low_lane)
            xm = jnp.where(keep, x, jnp.zeros_like(x))
            dym = jnp.where(keep, dy, jnp.zeros_like(dy))
            lc, lr, sc = lcol[0, 0][:, h : h + 1], lrow[0, 0][h : h + 1], scol[0, 0][:, h : h + 1]

            def piece(rows, cols, masked):
                differ = lr[:, cols] - lc[rows]
                if masked:
                    differ = jnp.where(causal, differ, -1e30)
                factor = jnp.exp(differ) * sc[rows]
                mixing = factor * scores[rows, cols]
                grad = mm_nt(xm[rows], dy[cols])
                scores_grad[rows, cols] += grad * factor
                both = grad * mixing
                return mixing.astype(BF16), jnp.sum(both, axis=1, keepdims=True), jnp.sum(both, axis=0, keepdims=True)

            m_aa, c_aa, r_aa = piece(a, a, True)
            m_ab, c_ab, r_ab = piece(a, b, False)
            m_bb, c_bb, r_bb = piece(b, b, True)
            upper = upper + mm(m_aa, dym[a]) + mm(m_ab, dym[b])
            lower = lower + mm(m_bb, dym[b])
            row_sum[0, 0, h : h + 1, a] = r_aa
            row_sum[0, 0, h : h + 1, b] = r_ab + r_bb
            col_sum[0, 0, a, h : h + 1] = c_aa + c_ab
            col_sum[0, 0, b, h : h + 1] = c_bb
        extra = dyf * skip[:, lanes]
        value_grad[0, a, lanes] = (upper + extra[a]).astype(BF16)
        value_grad[0, b, lanes] = (lower + extra[b]).astype(BF16)

    @pl.when(g == NB - 1)
    def _():
        sg = scores_grad[...]
        b_grad[0] = mm(sg.astype(BF16), bc[0][:, STATE:])
        c_grad[0] = mm(sg.T.astype(BF16), bc[0][:, :STATE])


def local(active, mixed_grad, lcol, lrow, scol, skip):
    seqs, length, _ = active.shape
    col = pl.BlockSpec((1, 1, length, HB), lambda s, g: (s, g, 0, 0))
    row = pl.BlockSpec((1, 1, HB, length), lambda s, g: (s, g, 0, 0))
    blk = pl.BlockSpec((1, length, LB), lambda s, g: (s, 0, g))
    one = pl.BlockSpec((1, length, STATE), lambda s, g: (s, 0, 0))
    return pl.pallas_call(
        local_kernel,
        grid=(seqs, NB),
        in_specs=[blk, blk, pl.BlockSpec((1, length, LB), lambda s, g: (s, 0, NB)), col, row, col, pl.BlockSpec((1, LB), lambda s, g: (0, g))],
        out_specs=[blk, row, col, one, one, pl.BlockSpec((1, 1, LB), lambda s, g: (s, 0, g))],
        out_shape=[
            jax.ShapeDtypeStruct((seqs, length, INNER), BF16),
            jax.ShapeDtypeStruct((seqs, NB, HB, length), F32),
            jax.ShapeDtypeStruct((seqs, NB, length, HB), F32),
            jax.ShapeDtypeStruct((seqs, length, STATE), F32),
            jax.ShapeDtypeStruct((seqs, length, STATE), F32),
            jax.ShapeDtypeStruct((seqs, 1, INNER), F32),
        ],
        scratch_shapes=[pltpu.VMEM((length, length), F32), pltpu.VMEM((length, length), F32)],
        cost_estimate=pl.CostEstimate(flops=40 * 10**9, bytes_accessed=12 * 10**6, transcendentals=6 * 10**6),
        name="local",
    )(active, mixed_grad, active, lcol, lrow, scol, skip)


def back_kernel(
    mixed, edge, taps, bias, values, bblock, value_grad, entry, leaving, entering, weigh, table, folded, b_own, c_own,
    mixed_grad, halo, tap_grad, bias_grad, weigh_grad, state_dot, bc_sum, weigh_sum,
):
    g = pl.program_id(1)
    conv, ext = convolve(mixed[0], edge[0], taps[...], bias[...])
    s = sigmoid(conv)
    slope = s * (1.0 + conv * (1.0 - s))
    length = conv.shape[0]

    @pl.when(g == 0)
    def _():
        bc_sum[:, :STATE] = b_own[0]
        bc_sum[:, STATE:] = c_own[0]
        weigh_sum[...] = jnp.zeros_like(weigh_sum)

    def finish(grad):
        cg = grad * slope
        bias_grad[0] = jnp.sum(cg, axis=0, keepdims=True)
        base = ext.shape[0] - length - KCONV + 1
        for k in range(KCONV):
            tap_grad[0, k : k + 1] = jnp.sum(cg * ext[base + k : base + k + length], axis=0, keepdims=True)
        zero = jnp.zeros((8, cg.shape[1]), F32)
        wide = jnp.concatenate([zero, cg, zero], axis=0)
        out = taps[0:1] * wide[11 : 11 + length]
        for k in range(1, KCONV):
            out = out + taps[k : k + 1] * wide[11 - k : 11 - k + length]
        mixed_grad[0] = out.astype(BF16)
        edge_out = taps[0:1] * wide[3:11]
        for k in range(1, KCONV):
            edge_out = edge_out + taps[k : k + 1] * wide[3 - k : 11 - k]
        halo[0] = edge_out

    @pl.when(g < NB)
    def _():
        x = values[0].astype(F32)
        w = spread(weigh[0], table[...])
        inner = mm(bblock[0], leaving[0])
        scaled = inner * w
        weigh_sum[...] += spread(scaled * x, folded[...])
        bc_sum[:, :STATE] += mm_nt((x * w).astype(BF16), leaving[0])
        bc_sum[:, STATE:] += mm_nt(entry[0], entering[0])
        state_dot[0] = jnp.sum(leaving[0].astype(F32) * entering[0].astype(F32), axis=0, keepdims=True)
        finish(value_grad[0].astype(F32) + scaled)

    @pl.when(g == NB)
    def _():
        finish(bc_sum[...])
        weigh_grad[0] = weigh_sum[...]


def back(mixed, edge, taps, bias, active, value_grad, entry, leaving, entering, weigh, table, folded, b_own, c_own):
    seqs, length, _ = active.shape
    held = lambda g: jnp.minimum(g, NB - 1)
    blk = pl.BlockSpec((1, length, LB), lambda s, g: (s, 0, g))
    inner = pl.BlockSpec((1, length, LB), lambda s, g: (s, 0, held(g)))
    st = pl.BlockSpec((1, STATE, LB), lambda s, g: (s, 0, held(g)))
    one = pl.BlockSpec((1, length, STATE), lambda s, g: (s, 0, 0))
    return pl.pallas_call(
        back_kernel,
        grid=(seqs, NB + 1),
        in_specs=[
            blk,
            pl.BlockSpec((1, 8, LB), lambda s, g: (s, 0, g)),
            pl.BlockSpec((KCONV, LB), lambda s, g: (0, g)),
            pl.BlockSpec((1, LB), lambda s, g: (0, g)),
            inner,
            pl.BlockSpec((1, length, STATE), lambda s, g: (s, 0, INNER // STATE)),
            inner,
            inner,
            st,
            st,
            pl.BlockSpec((1, length, HEADS), lambda s, g: (s, 0, 0)),
            pl.BlockSpec((HEADS, LB), lambda s, g: (0, held(g))),
            pl.BlockSpec((LB, HEADS), lambda s, g: (held(g), 0)),
            one,
            one,
        ],
        out_specs=[
            blk,
            pl.BlockSpec((1, 8, LB), lambda s, g: (s, 0, g)),
            pl.BlockSpec((1, KCONV, LB), lambda s, g: (s, 0, g)),
            pl.BlockSpec((1, 1, LB), lambda s, g: (s, 0, g)),
            pl.BlockSpec((1, length, HEADS), lambda s, g: (s, 0, 0)),
            pl.BlockSpec((1, 1, LB), lambda s, g: (s, 0, held(g))),
        ],
        out_shape=[
            jax.ShapeDtypeStruct((seqs, length, CONVCH), BF16),
            jax.ShapeDtypeStruct((seqs, 8, CONVCH), F32),
            jax.ShapeDtypeStruct((seqs, KCONV, CONVCH), F32),
            jax.ShapeDtypeStruct((seqs, 1, CONVCH), F32),
            jax.ShapeDtypeStruct((seqs, length, HEADS), F32),
            jax.ShapeDtypeStruct((seqs, 1, INNER), F32),
        ],
        scratch_shapes=[pltpu.VMEM((length, 2 * STATE), F32), pltpu.VMEM((length, HEADS), F32)],
        cost_estimate=pl.CostEstimate(flops=4 * 10**9, bytes_accessed=24 * 10**6, transcendentals=2 * 10**6),
        name="back",
    )(mixed, edge, taps, bias, active, active, value_grad, entry, leaving, entering, weigh, table, folded, b_own, c_own)


def contract_rows(left, right):
    return lax.dot_general(left, right, (((0,), (0,)), ((), ())), preferred_element_type=F32)


def shards(
    activations,
    gate_weight,
    mixer_weight,
    step_weight,
    out_weight,
    conv_weight,
    conv_bias,
    norm_gain,
    gate_gain,
    step_bias,
    decay_log,
    skip_gain,
    cotangent,
):
    grid = Grid()
    parts = grid.dp * grid.seq
    seqs, length, model = activations.shape
    tokens = seqs * length
    rows = mixer_weight.shape[0]
    chans, gains = conv_bias.shape[0], gate_gain.shape[0]
    small = jnp.concatenate([norm_gain, gate_gain, conv_bias, conv_weight.reshape(-1)])
    room = PACKED - CONVCH - HEADS
    small = jnp.pad(small, (0, rows * room - small.shape[0])).reshape(rows, room)
    packed = jnp.concatenate([mixer_weight, step_weight, small], axis=1)
    full_mixer = lax.all_gather(packed, ("dp", "seq"), axis=0, tiled=True)
    full_out = lax.all_gather(out_weight, ("dp", "seq"), axis=0, tiled=True)
    full_gate = lax.all_gather(gate_weight, ("dp", "seq"), axis=0, tiled=True)

    smalls = full_mixer[:, CONVCH + HEADS :].reshape(parts, rows * room).astype(F32)
    offset = 0
    full_norm = smalls[:, offset : offset + rows].reshape(1, model)
    offset += rows
    full_gain = smalls[:, offset : offset + gains].reshape(1, INNER)
    offset += gains
    full_bias = smalls[:, offset : offset + chans].reshape(1, CONVCH)
    offset += chans
    full_taps = smalls[:, offset : offset + KCONV * chans].reshape(parts, KCONV, chans)
    full_taps = full_taps.transpose(1, 0, 2).reshape(KCONV, CONVCH)

    source = activations.astype(F32).reshape(tokens, model)
    scaling = lax.rsqrt(jnp.mean(source * source, axis=-1, keepdims=True) + epsilon)
    normed = (source * scaling * full_norm).astype(BF16)
    tangent = cotangent.reshape(tokens, model)

    mixed = jnp.dot(normed, full_mixer, preferred_element_type=F32).reshape(seqs, length, PACKED)
    edge = shifted(mixed[:, length - KCONV + 1 :, :CONVCH], "seq", 1)
    edge = jnp.pad(edge, ((0, 0), (8 - KCONV + 1, 0), (0, 0)))
    raw = mixed[:, :, CONVCH : CONVCH + HEADS] + step_bias
    steps = jax.nn.softplus(raw)
    decay_rate = jnp.exp(decay_log)
    log_decay = -decay_rate * steps
    triangle = jnp.tril(jnp.ones((length, length), F32))
    cumulative = jnp.einsum("ij,sjh->sih", triangle, log_decay, precision=precise)
    ending = cumulative[:, -1:, :]
    weigh = jnp.exp(ending - cumulative) * steps
    grown = jnp.exp(cumulative)
    head_of = lax.broadcasted_iota(jnp.int32, (HEADS, INNER), 1) // HDIM
    table = (head_of == lax.broadcasted_iota(jnp.int32, (HEADS, INNER), 0)).astype(BF16)
    folded = table.T
    block_decay = jnp.dot(jnp.exp(ending[:, 0]), table.astype(F32), precision=precise)
    skip_wide = jnp.dot(skip_gain[None], table.astype(F32), precision=precise)

    def as_cols(v):
        return v.reshape(seqs, length, NB, HB).transpose(0, 2, 1, 3)

    def as_rows(v):
        return v.reshape(seqs, length, NB, HB).transpose(0, 2, 3, 1)

    lcol, lrow, scol, srow = as_cols(cumulative), as_rows(cumulative), as_cols(steps), as_rows(steps)
    active, fresh = front(mixed, edge, full_taps, full_bias, weigh, table)
    entering = jnp.stack([carried_in(grid, fresh[s], block_decay[s : s + 1], False) for s in range(seqs)])
    own = inside(active, lcol, lrow, srow, skip_wide)
    gate_z = jnp.dot(normed, full_gate, preferred_element_type=F32).reshape(seqs, length, INNER)
    top = lax.dot_general(tangent, full_out, (((1,), (1,)), ((), ())), preferred_element_type=F32)
    gnorm, gate_grad, mixed_grad, entry, carry_grad, gain_grad = gate(
        own, gate_z, top.reshape(seqs, length, INNER), active, entering, grown, table, folded, full_gain
    )

    inputs_c = active[:, :, INNER + STATE :]
    entry_grad = jnp.einsum("sin,sif->snf", inputs_c, entry, preferred_element_type=F32).astype(BF16)
    leaving = jnp.stack([carried_in(grid, entry_grad[s], block_decay[s : s + 1], True) for s in range(seqs)])

    def by_core(value):
        def pick(core):
            split = value.reshape(tokens, grid.size["y"], 2, value.shape[1] // (2 * grid.size["y"]))
            return lax.dynamic_index_in_dim(split, core, 2, False).reshape(tokens, value.shape[1] // 2)

        return pick

    gnorm = gnorm.reshape(tokens, INNER)
    gate_grad = gate_grad.reshape(tokens, INNER)
    gnorm_of, normed_of = by_core(gnorm), by_core(normed)
    out_w_grad = scatter_sum(grid, lambda core: contract_rows(gnorm_of(core), tangent), out_weight.shape[0], model)
    gate_w_grad = scatter_sum(grid, lambda core: contract_rows(normed_of(core), gate_grad), rows, INNER)
    projected = jnp.dot(gnorm, full_out, preferred_element_type=F32)
    output = (source + projected).astype(BF16).reshape(seqs, length, model)

    value_grad, row_sum, col_sum, b_own, c_own, skip_part = local(active, mixed_grad, lcol, lrow, scol, skip_wide)
    mixer_grad, halo, tap_grad, bias_grad, weigh_grad, state_dot = back(
        mixed, edge, full_taps, full_bias, active, value_grad, entry, leaving, entering, weigh, table, folded, b_own, c_own
    )
    halo_grad = shifted(halo[:, 8 - KCONV + 1 :].astype(BF16), "seq", -1)
    tail = mixer_grad[:, length - KCONV + 1 :].astype(F32) + halo_grad.astype(F32)
    mixer_grad = lax.dynamic_update_slice(mixer_grad, tail.astype(BF16), (0, length - KCONV + 1, 0))

    row_sum = row_sum.transpose(0, 3, 1, 2).reshape(seqs, length, HEADS)
    col_sum = col_sum.transpose(0, 2, 1, 3).reshape(seqs, length, HEADS)
    scaled_step = col_sum + weigh_grad
    end_grad = jnp.sum(weigh_grad, axis=1) + jnp.exp(ending[:, 0]) * jnp.dot(
        state_dot[:, 0], folded.astype(F32), precision=precise
    )
    level_grad = row_sum - scaled_step + carry_grad
    decay_grad = jnp.einsum("ji,sjh->sih", triangle, level_grad, precision=precise) + end_grad[:, None]
    sig = jax.nn.sigmoid(raw)
    ratio = jnp.where(raw < -15.0, 1.0, sig / jnp.where(raw < -15.0, 1.0, steps))
    raw_grad = scaled_step * ratio - decay_rate * decay_grad * sig
    bias_step = jnp.sum(raw_grad, axis=(0, 1))
    decay_total = jnp.sum(decay_grad * log_decay, axis=(0, 1))
    skip_total = jnp.dot(jnp.sum(skip_part, axis=(0, 1))[None], folded.astype(F32), precision=precise)[0]

    mixer_grad = jnp.concatenate(
        [
            mixer_grad.reshape(tokens, CONVCH),
            raw_grad.astype(BF16).reshape(tokens, HEADS),
            jnp.zeros((tokens, room), BF16),
        ],
        axis=1,
    )
    mixer_w_grad = scatter_sum(grid, lambda core: contract_rows(normed_of(core), mixer_grad), rows, PACKED)
    normed_grad = lax.dot_general(
        gate_grad, full_gate, (((1,), (1,)), ((), ())), preferred_element_type=F32
    ) + lax.dot_general(mixer_grad, full_mixer, (((1,), (1,)), ((), ())), preferred_element_type=F32)
    v = source * scaling
    norm_part = jnp.sum(normed_grad * v, axis=0)
    scaled_grad = normed_grad * full_norm
    input_grad = cotangent.astype(F32).reshape(tokens, model) + scaling * (
        scaled_grad - v * jnp.mean(scaled_grad * v, axis=-1, keepdims=True)
    )

    tap_total = jnp.sum(tap_grad, axis=0).reshape(KCONV, parts, chans).transpose(1, 0, 2).reshape(parts, KCONV * chans)
    owned = jnp.concatenate(
        [
            norm_part.reshape(parts, rows),
            gain_grad.reshape(parts, gains),
            jnp.sum(bias_grad, axis=(0, 1)).reshape(parts, chans),
            tap_total,
        ],
        axis=1,
    )
    width = owned.shape[1]
    summed = total_of(grid, jnp.concatenate([owned.reshape(-1), bias_step, decay_total, skip_total]))
    me = lax.axis_index("dp") * grid.seq + lax.axis_index("seq")
    mine = lax.dynamic_slice(summed, (me * width,), (width,))
    heads = summed[parts * width :]
    o1, o2, o3 = rows, rows + gains, rows + gains + chans
    return (
        output,
        input_grad.reshape(seqs, length, model),
        gate_w_grad,
        mixer_w_grad[:, :CONVCH],
        mixer_w_grad[:, CONVCH : CONVCH + HEADS],
        out_w_grad,
        mine[o3:].reshape(KCONV, chans),
        mine[o2:o3],
        mine[:o1],
        mine[o1:o2],
        heads[:HEADS],
        heads[HEADS : 2 * HEADS],
        heads[2 * HEADS :],
    )


def solution(mesh):
    both = ("dp", "seq")
    return jax.shard_map(
        shards,
        mesh=mesh,
        in_specs=(
            P("dp", "seq", None),
            P(both, None),
            P(both, None),
            P(both, None),
            P(both, None),
            P(None, both),
            P(both),
            P(both),
            P(both),
            P(),
            P(),
            P(),
            P("dp", "seq", None),
        ),
        out_specs=(
            P("dp", "seq", None),
            P("dp", "seq", None),
            P(both, None),
            P(both, None),
            P(both, None),
            P(both, None),
            P(None, both),
            P(both),
            P(both),
            P(both),
            P(),
            P(),
            P(),
        ),
        check_vma=False,
    )
```
